32 devices in a mesh: fsdp: 4 (over x, core), tok: 8 (over z, y).
Axes of the slice: x: 2, y: 2, z: 4, core: 2. Of those that a mesh axis runs over, the one named last changes fastest.
Arguments:
- states: bfloat16 [4, 512, 1024], P('fsdp', 'tok'), may hold values from -8 to 8
- cache_keys: bfloat16 [4, 1024, 1024], P('fsdp', 'tok'), may hold values from -6 to 6
- cache_values: bfloat16 [4, 1024, 1024], P('fsdp', 'tok'), may hold values from -6 to 6
- cache_len: int32 [4], P('fsdp'), may hold values from 1 to 1024, as said below
- token_slot: int32 [4, 512], P('fsdp', 'tok'), may hold values from 0 to 511, as said below
- bucket_table: int32 [1536], replicated, may hold values from 0 to 31
- rel_bias: float32 [32, 16], replicated, may hold values from -3 to 250
- norm_gain: float32 [1024], replicated, may hold values from 0.5 to 1.5
- w_query: bfloat16 [1024, 1024], P(('fsdp', 'tok')), may hold values from -0.0234375 to 0.0234375
- w_key: bfloat16 [1024, 1024], P(('fsdp', 'tok')), may hold values from -0.1875 to 0.1875
- w_value: bfloat16 [1024, 1024], P(('fsdp', 'tok')), may hold values from -0.1875 to 0.1875
- w_out: bfloat16 [1024, 1024], P(('fsdp', 'tok')), may hold values from -1.5 to 1.5
Outputs:
- hidden_out: bfloat16 [4, 512, 1024], P('fsdp', 'tok')
- new_keys: bfloat16 [4, 512, 1024], P('fsdp', 'tok')
- new_values: bfloat16 [4, 512, 1024], P('fsdp', 'tok')
The draws below stay inside these ranges and needn't reach their ends.
Inputs may be any that keep to these rules, and one draw needn't show every extreme that they name: `cache_len`: one request has exactly 1024 live rows. `token_slot`: each row is a permutation of 0 to 511; every aligned block of 64 tokens of a request has exactly 8 of its slots in each aligned block of 64 slots.
All inputs are finite; a program needn't handle non-finite values.
Results may differ from the reference program's by a relative error of at most 0.0095.
Values may be sent and summed in bfloat16 or wider, within the bound.
No kernel may reach another device: no remote copies, remote signals or barrier semaphores. Data moves between devices by JAX's collectives and lax.ppermute only.
A program may use at most 64 MiB of HBM per device.

```python
import jax
import jax.numpy as jnp
from jax import lax

D = 1024
HEADS = 16
HEAD_DIM = 64
BUCKETS = 32
TOK_DEV = 64
REQUESTS = 4
NEW = 512
CACHE = 1024
REL = 1536


def draw_states(key, part):
    first, second, third = jax.random.split(key, 3)
    row_scale = jnp.exp(jax.random.uniform(second, (REQUESTS, NEW, 1), minval=jnp.log(0.3), maxval=jnp.log(3.0)))
    col_scale = jnp.exp(jax.random.uniform(third, (1, 1, D), minval=jnp.log(0.3), maxval=jnp.log(3.0)))
    drawn = jax.random.normal(first, (REQUESTS, NEW, D)) * row_scale * col_scale
    return jnp.clip(drawn.astype(jnp.float32), -8.0, 8.0).astype(jnp.bfloat16)


def draw_rel_bias(key, part):
    first = jax.random.fold_in(key, 0)
    base_vals = jax.random.uniform(first, (BUCKETS, HEADS), minval=-3.0, maxval=3.0)
    drawn = base_vals
    return drawn.astype(jnp.float32)


def draw_cache_len(key, part):
    first, second, third, fourth = jax.random.split(jax.random.fold_in(key, 5), 4)
    lengths = jax.random.randint(first, (REQUESTS,), 1, CACHE + 1)
    longest = jax.random.randint(second, (), 0, REQUESTS)
    shortest = (longest + 1 + jax.random.randint(third, (), 0, REQUESTS - 1)) % REQUESTS
    short_len = jnp.minimum(jax.random.randint(fourth, (), 1, 17), CACHE)
    indices = jnp.arange(REQUESTS)
    lengths = jnp.where(indices == shortest, short_len, lengths)
    lengths = jnp.where(indices == longest, CACHE, lengths)
    return lengths.astype(jnp.int32)


def draw_token_slot(key, part):
    blocks = NEW // TOK_DEV
    per_peer = TOK_DEV // blocks
    source_keys = jax.random.split(jax.random.fold_in(key, 11), REQUESTS * blocks)
    target_keys = jax.random.split(jax.random.fold_in(key, 12), REQUESTS * blocks)
    source_perm = jax.vmap(lambda one_key: jax.random.permutation(one_key, TOK_DEV))(source_keys).reshape(REQUESTS, blocks, TOK_DEV)
    target_perm = jax.vmap(lambda one_key: jax.random.permutation(one_key, TOK_DEV))(target_keys).reshape(REQUESTS, blocks * TOK_DEV)
    target_dev = source_perm // per_peer
    within = source_perm % per_peer
    source_idx = jnp.arange(blocks, dtype=jnp.int32)[None, :, None]
    entry_idx = source_idx * per_peer + within
    local_slot = jnp.take_along_axis(target_perm, (target_dev * TOK_DEV + entry_idx).reshape(REQUESTS, -1), axis=1)
    slot_ids = target_dev.reshape(REQUESTS, -1) * TOK_DEV + local_slot
    return slot_ids.astype(jnp.int32)


def draw_bucket_table(key, part):
    distance = jnp.arange(REL, dtype=jnp.int32)
    coin = jax.random.randint(jax.random.fold_in(key, 7), (REL,), 0, jnp.maximum(distance, 1))
    stepped = jnp.where(distance < 16, (distance > 0).astype(jnp.int32), (coin < 3).astype(jnp.int32))
    table = jnp.minimum(jnp.cumsum(stepped), BUCKETS - 1)
    table = jnp.where(distance == REL - 1, BUCKETS - 1, table)
    return table.astype(jnp.int32)


def block_levels(key, dims, cuts, least, largest):
    factor_of = 1.0
    for axis_at, blocks in cuts:
        draws = jax.random.uniform(jax.random.fold_in(jax.random.fold_in(key, 6), axis_at), (blocks,), jnp.float32, least / len(cuts), largest / len(cuts))
        factor_of = factor_of * jnp.repeat(jnp.exp(draws), dims[axis_at] // blocks).reshape((-1,) + (1,) * (len(dims) - 1 - axis_at))
    return factor_of


def gaussian(own_key, extent, deviation, bound, cuts=(), held_as=jnp.bfloat16):
    array = deviation * jax.random.normal(own_key, extent, jnp.float32)
    if cuts:
        array = array * block_levels(own_key, extent, cuts, -0.22, 0.18)
    return jnp.clip(array, -bound, bound).astype(held_as)


def setup_inputs(seed: int = 0) -> dict:
    arg_keys = jax.random.split(jax.random.key(seed), 13)
    states = draw_states(jax.random.fold_in(arg_keys[12], 71), 0)
    cache_keys = gaussian(arg_keys[1], (REQUESTS, CACHE, D), 1.0, 6.0, ((0, 4), (1, 8)))
    cache_values = gaussian(arg_keys[2], (REQUESTS, CACHE, D), 1.0, 6.0, ((0, 4), (1, 8)))
    cache_len = draw_cache_len(jax.random.fold_in(arg_keys[12], 71), 0)
    token_slot = draw_token_slot(jax.random.fold_in(arg_keys[12], 71), 0)
    bucket_table = draw_bucket_table(jax.random.fold_in(arg_keys[12], 71), 0)
    rel_bias = draw_rel_bias(jax.random.fold_in(arg_keys[12], 71), 0)
    norm_gain = jnp.clip(1.0 + 0.1 * jax.random.normal(arg_keys[7], (D,), jnp.float32), 0.5, 1.5)
    w_query = gaussian(arg_keys[8], (D, D), (64 * D) ** -0.5, 0.0234375, ((0, 32),))
    w_key = gaussian(arg_keys[9], (D, D), D ** -0.5, 0.1875, ((0, 32),))
    w_value = gaussian(arg_keys[10], (D, D), D ** -0.5, 0.1875, ((0, 32),))
    w_out = gaussian(arg_keys[11], (D, D), (D // 64) ** -0.5, 1.5, ((0, 32),))
    return dict(states=states, cache_keys=cache_keys, cache_values=cache_values, cache_len=cache_len, token_slot=token_slot, bucket_table=bucket_table, rel_bias=rel_bias, norm_gain=norm_gain, w_query=w_query, w_key=w_key, w_value=w_value, w_out=w_out)


far_away = 1073741824

def reference(states, cache_keys, cache_values, cache_len, token_slot, bucket_table, rel_bias, norm_gain, w_query, w_key, w_value, w_out):
    bias_table = rel_bias[bucket_table]

    def one_request(request):
        tokens, old_keys, old_values, length, slot_ids = request
        wide_in = tokens.astype(jnp.float32)
        inverse = lax.rsqrt(lax.optimization_barrier(jnp.mean(wide_in * wide_in, axis=-1, keepdims=True)) + 1e-06)
        normed = (wide_in * inverse * norm_gain).astype(jnp.bfloat16)
        queries = jnp.dot(normed, w_query, preferred_element_type=jnp.float32).astype(jnp.bfloat16)
        fresh_keys = jnp.dot(normed, w_key, preferred_element_type=jnp.float32).astype(jnp.bfloat16)
        fresh_values = jnp.dot(normed, w_value, preferred_element_type=jnp.float32).astype(jnp.bfloat16)
        all_keys = jnp.concatenate([old_keys, fresh_keys]).astype(jnp.float32).reshape(CACHE + NEW, HEADS, HEAD_DIM)
        all_values = jnp.concatenate([old_values, fresh_values]).astype(jnp.float32).reshape(CACHE + NEW, HEADS, HEAD_DIM)
        cache_spot = jnp.arange(CACHE, dtype=jnp.int32)
        query_pos = length + jnp.arange(NEW, dtype=jnp.int32)
        key_pos = jnp.concatenate([jnp.where(cache_spot < length, cache_spot, far_away), query_pos])
        blocks_q = queries.astype(jnp.float32).reshape(NEW // TOK_DEV, TOK_DEV, HEADS, HEAD_DIM)
        blocks_pos = query_pos.reshape(NEW // TOK_DEV, TOK_DEV)

        def attend(block_set):
            query_block, pos_block = block_set
            scores = jnp.einsum('qhd,khd->hqk', query_block, all_keys)
            distance = pos_block[:, None] - key_pos[None, :]
            bias_add = jnp.take(bias_table, jnp.clip(distance, 0, REL - 1), axis=0)
            scores = scores + jnp.transpose(bias_add, (2, 0, 1))
            scores = jnp.where((distance >= 0)[None], scores, -jnp.inf)
            weights = jax.nn.softmax(scores, axis=-1).astype(jnp.bfloat16)
            context = jnp.einsum('hqk,khd->qhd', weights.astype(jnp.float32), all_values)
            return context.reshape(query_block.shape[0], D).astype(jnp.bfloat16)
        context = lax.map(attend, (blocks_q, blocks_pos)).reshape(NEW, D)
        result = (wide_in + jnp.dot(context, w_out, preferred_element_type=jnp.float32)).astype(jnp.bfloat16)
        placed_keys = jnp.zeros_like(fresh_keys).at[slot_ids].set(fresh_keys)
        placed_values = jnp.zeros_like(fresh_values).at[slot_ids].set(fresh_values)
        return (result, placed_keys, placed_values)
    hidden_out, new_keys, new_values = lax.map(one_request, (states, cache_keys, cache_values, cache_len, token_slot))
    return (hidden_out, new_keys, new_values)
```

```python
import functools

import jax
import jax.numpy as jnp
from jax import lax
from jax.experimental import pallas as pl
from jax.experimental.pallas import tpu as pltpu
from jax.sharding import PartitionSpec as P

masked = -1e30
q_rows = 128
lanes = 128
slot_base = 32
vmem_bytes = 32 * 1024 * 1024


def bias_rows(bucket_table, head_bias, new_count):
    buckets = jnp.arange(head_bias.shape[1], dtype=jnp.int32)

    def look_up(table):
        hit = table[None, None, :] == buckets[None, :, None]
        return jnp.sum(jnp.where(hit, head_bias[:, :, None], 0.0), axis=1)

    first = new_count - q_rows
    cache_order = jnp.concatenate(
        [jnp.flip(bucket_table[: first + 1]), jnp.flip(bucket_table[first + 1 :])]
    )
    new_order = jnp.concatenate(
        [
            jnp.flip(bucket_table[: first + 1]),
            jnp.full((new_count,), -1, jnp.int32),
            jnp.flip(bucket_table[first + 1 : new_count]),
        ]
    )
    new_bias = jnp.where((new_order < 0)[None], masked, look_up(new_order))
    return look_up(cache_order), new_bias


def qkv_kernel(place_ref, x_ref, w_ref, q_ref, k_ref, v_ref):
    width = q_ref.shape[1]
    count = place_ref.shape[0]
    rows = x_ref.shape[0] // count
    for part, out in enumerate((q_ref, k_ref, v_ref)):
        made = jnp.dot(
            x_ref[...],
            w_ref[:, part * width : (part + 1) * width],
            preferred_element_type=jnp.float32,
        ).astype(jnp.bfloat16)
        for block in range(count):
            spot = pl.multiple_of(place_ref[block] * rows, rows)
            out[pl.ds(spot, rows), :] = made[block * rows : (block + 1) * rows]


def table_kernel(len_ref, cache_row_ref, new_row_ref, cache_tab, new_tab):
    for row_ref, tab, shift in ((cache_row_ref, cache_tab, len_ref[0]), (new_row_ref, new_tab, None)):
        span = tab.shape[2]
        for h in range(tab.shape[0]):
            base = jnp.broadcast_to(row_ref[h : h + 1, :], (8, span))
            if shift is not None:
                base = pltpu.roll(base, shift, 1)
            row = lax.broadcasted_iota(jnp.int32, (8, span), 0)
            for bit in (1, 2, 4):
                base = jnp.where((row & bit) != 0, pltpu.roll(base, bit, 1), base)
            for group in range(tab.shape[1] // 8):
                tab[h, group * 8 : (group + 1) * 8, :] = (
                    pltpu.roll(base, group * 8, 1) if group else base
                )


def attend_kernel(
    head_count,
    head_size,
    len_ref,
    q_ref,
    k_ref,
    v_ref,
    cache_ref,
    cache_tab,
    new_tab,
    slots_ref,
    out_ref,
    key_aug,
    val_aug,
    new_val_aug,
):
    peers = out_ref.shape[0]
    tok_rows = out_ref.shape[1] // 3
    new_count = q_ref.shape[0]
    width = q_ref.shape[1]
    cache_rows = (cache_ref.shape[1] - 8) // 2
    cache_count = peers * cache_rows
    length = len_ref[0]

    old_keys = cache_ref[:, :cache_rows, :].reshape(cache_count, width)
    old_vals = cache_ref[:, cache_rows : 2 * cache_rows, :].reshape(cache_count, width)
    key_row = lax.broadcasted_iota(jnp.int32, (cache_count, width), 0)
    key_lane = lax.broadcasted_iota(jnp.int32, (cache_count, width), 1)
    new_lane = lax.broadcasted_iota(jnp.int32, (new_count, width), 1)
    dead = jnp.where(key_row < length, 0.0, masked).astype(jnp.bfloat16)
    one = jnp.ones((), jnp.bfloat16)
    for h in range(head_count):
        spare = ((h + 1) * head_size) % width
        mine = (key_lane >= h * head_size) & (key_lane < (h + 1) * head_size)
        mine_new = (new_lane >= h * head_size) & (new_lane < (h + 1) * head_size)
        key_aug[h] = jnp.where(key_lane == spare, dead, old_keys)
        val_aug[h] = jnp.where(mine, old_vals, one)
        new_val_aug[h] = jnp.where(mine_new, v_ref[...], one)

    lane = lax.broadcasted_iota(jnp.int32, (q_rows, width), 1)
    per_dest = tok_rows
    for block in range(new_count // q_rows):
        q_here = q_ref[block * q_rows : (block + 1) * q_rows, :]
        start = new_count - q_rows - block * q_rows
        seen = (block + 1) * q_rows
        made = None
        for h in range(head_count):
            spare = ((h + 1) * head_size) % width
            mine = (lane >= h * head_size) & (lane < (h + 1) * head_size)
            q_new = jnp.where(mine, q_here, jnp.zeros((), jnp.bfloat16))
            q_old = jnp.where(lane == spare, one, q_new)
            s_old = lax.dot_general(
                q_old, key_aug[h], (((1,), (1,)), ((), ())), preferred_element_type=jnp.float32
            )
            s_new = lax.dot_general(
                q_new,
                k_ref[:seen, :],
                (((1,), (1,)), ((), ())),
                preferred_element_type=jnp.float32,
            )
            s_old = s_old + cache_tab[h, :, start : start + cache_count]
            s_new = s_new + new_tab[h, :, start : start + seen]
            peak = jnp.maximum(
                jnp.max(s_old, axis=1, keepdims=True), jnp.max(s_new, axis=1, keepdims=True)
            )
            p_old = jnp.exp(s_old - peak).astype(jnp.bfloat16)
            p_new = jnp.exp(s_new - peak).astype(jnp.bfloat16)
            total = jnp.dot(p_old, val_aug[h], preferred_element_type=jnp.float32) + jnp.dot(
                p_new, new_val_aug[h, :seen, :], preferred_element_type=jnp.float32
            )
            part = total / total[:, spare : spare + 1]
            made = part if made is None else jnp.where(mine, part, made)
        made = made.astype(jnp.bfloat16)
        for piece in range(q_rows // per_dest):
            out_ref[block * (q_rows // per_dest) + piece, :per_dest, :] = made[
                piece * per_dest : (piece + 1) * per_dest
            ]

    slot_row = lax.broadcasted_iota(jnp.int32, (new_count, new_count), 0)
    deal = (slots_ref[...] == slot_row).astype(jnp.bfloat16)
    for part, ref in ((1, k_ref), (2, v_ref)):
        dealt = jnp.dot(deal, ref[...], preferred_element_type=jnp.float32).astype(jnp.bfloat16)
        for dest in range(peers):
            out_ref[dest, part * tok_rows : (part + 1) * tok_rows, :] = dealt[
                dest * tok_rows : (dest + 1) * tok_rows
            ]


def finish_kernel(got_ref, w_ref, states_ref, hidden_ref, keys_ref, values_ref):
    peers = got_ref.shape[0]
    rows = states_ref.shape[0]
    context = jnp.concatenate([got_ref[p, :rows, :] for p in range(peers)], axis=1)
    keys_ref[...] = jnp.concatenate([got_ref[p, rows : 2 * rows, :] for p in range(peers)], axis=1)
    values_ref[...] = jnp.concatenate(
        [got_ref[p, 2 * rows : 3 * rows, :] for p in range(peers)], axis=1
    )
    hidden_ref[...] = (
        states_ref[...].astype(jnp.float32)
        + jnp.dot(context, w_ref[...], preferred_element_type=jnp.float32)
    ).astype(jnp.bfloat16)


def vmem():
    return pl.BlockSpec(memory_space=pltpu.VMEM)


def smem():
    return pl.BlockSpec(memory_space=pltpu.SMEM)


def call(kernel, outs, specs, scratch, name, flops, moved, kind=jnp.bfloat16):
    return pl.pallas_call(
        kernel,
        out_shape=[jax.ShapeDtypeStruct(shape, kind) for shape in outs],
        in_specs=specs,
        out_specs=[vmem() for unused in outs],
        scratch_shapes=scratch,
        name=name,
        cost_estimate=pl.CostEstimate(flops=flops, bytes_accessed=moved, transcendentals=0),
        compiler_params=pltpu.CompilerParams(vmem_limit_bytes=vmem_bytes),
    )


def shards(
    near,
    states,
    cache_keys,
    cache_values,
    cache_len,
    token_slot,
    bucket_table,
    rel_bias,
    norm_gain,
    w_query,
    w_key,
    w_value,
    w_out,
):
    peers = lax.axis_size("tok")
    me = lax.axis_index("tok")
    tokens = states[0]
    tok_rows, features = tokens.shape
    heads = rel_bias.shape[1]
    head_size = features // heads
    width = features // peers
    my_heads = width // head_size
    new_count = tok_rows * peers
    cache_rows = cache_keys.shape[1]

    out_w = lax.all_gather(w_out, ("fsdp", "tok"), axis=0, tiled=True)

    sent_w = jnp.stack([w_query, w_key, w_value], axis=1).reshape(-1, 3, peers, width)
    sent_w = jnp.transpose(sent_w, (2, 0, 1, 3)).reshape(peers, -1, 3 * width)
    got_w = lax.all_to_all(sent_w, "tok", split_axis=0, concat_axis=0, tiled=True)
    my_w = lax.all_gather(got_w.reshape(-1, 3 * width), "fsdp", axis=0, tiled=True)

    wide_in = tokens.astype(jnp.float32)
    inverse = lax.rsqrt(jnp.mean(wide_in * wide_in, axis=-1, keepdims=True) + 1e-06)
    normed = (wide_in * inverse * norm_gain).astype(jnp.bfloat16)
    far = peers // near
    parts, place = [], []
    for step in range(far):
        pairs = [(t, (t + near * step) % peers) for t in range(peers)]
        parts.append(lax.ppermute(normed, "tok", pairs) if step else normed)
        place.append((me + peers - near * step) % peers)
    for turn in range(1, near):
        for step in range(far):
            pairs = [(t, t - t % near + (t + turn) % near) for t in range(peers)]
            parts.append(lax.ppermute(parts[step], "tok", pairs))
            origin = place[step]
            place.append(origin - origin % near + (origin + near - turn) % near)
    gathered = jnp.concatenate(parts)
    place = jnp.stack(place).astype(jnp.int32)

    def columns(rows):
        return jnp.transpose(rows.reshape(-1, peers, width), (1, 0, 2))

    slots = token_slot[0]
    note = jnp.zeros((8, width), jnp.bfloat16)
    note = note.at[0, :tok_rows].set((slots // slot_base).astype(jnp.bfloat16))
    note = note.at[1, :tok_rows].set((slots % slot_base).astype(jnp.bfloat16))
    sent_cache = jnp.concatenate(
        [
            columns(cache_keys[0]),
            columns(cache_values[0]),
            jnp.broadcast_to(note[None], (peers, 8, width)),
        ],
        axis=1,
    )
    cache = lax.all_to_all(sent_cache, "tok", split_axis=0, concat_axis=0, tiled=True)
    notes = cache[:, 2 * cache_rows : 2 * cache_rows + 2, :tok_rows].astype(jnp.int32)
    all_slots = (notes[:, 0] * slot_base + notes[:, 1]).reshape(1, new_count)

    my_bias = jnp.transpose(lax.dynamic_slice_in_dim(rel_bias, me * my_heads, my_heads, axis=1))
    cache_bias, new_bias = bias_rows(bucket_table, my_bias, new_count)

    cache_tab, new_tab = call(
        table_kernel,
        [(my_heads, q_rows, row.shape[1]) for row in (cache_bias, new_bias)],
        [smem(), vmem(), vmem()],
        [],
        "tables",
        0,
        4 * my_heads * q_rows * (cache_bias.shape[1] + new_bias.shape[1]),
        jnp.float32,
    )(cache_len, cache_bias, new_bias)

    queries, keys, values = call(
        qkv_kernel,
        [(new_count, width)] * 3,
        [smem(), vmem(), vmem()],
        [],
        "qkv",
        6 * new_count * features * width,
        2 * features * (new_count + 3 * width),
    )(place, gathered, my_w)

    if width < lanes:
        pad = ((0, 0), (0, lanes - width))
        queries, keys, values = (jnp.pad(one, pad) for one in (queries, keys, values))
        cache = jnp.pad(cache, ((0, 0),) + pad)
    full = max(width, lanes)
    (sent,) = call(
        functools.partial(attend_kernel, my_heads, head_size),
        [(peers, 3 * tok_rows, full)],
        [smem()] + [vmem()] * 7,
        [
            pltpu.VMEM((my_heads, peers * cache_rows, full), jnp.bfloat16),
            pltpu.VMEM((my_heads, peers * cache_rows, full), jnp.bfloat16),
            pltpu.VMEM((my_heads, new_count, full), jnp.bfloat16),
        ],
        "attend",
        4 * my_heads * new_count * (new_count + peers * cache_rows) * full,
        2 * full * (3 * new_count + 2 * peers * cache_rows),
    )(cache_len, queries, keys, values, cache, cache_tab, new_tab, all_slots)
    sent = sent[:, :, :width]

    got = lax.all_to_all(sent, "tok", split_axis=0, concat_axis=0, tiled=True)
    hidden, new_keys, new_values = call(
        finish_kernel,
        [(tok_rows, features)] * 3,
        [vmem()] * 3,
        [],
        "finish",
        2 * tok_rows * features * features,
        2 * features * (features + 5 * tok_rows),
    )(got, out_w, tokens)
    return (hidden[None], new_keys[None], new_values[None])


def solution(mesh):
    in_specs = (
        P("fsdp", "tok", None),
        P("fsdp", "tok", None),
        P("fsdp", "tok", None),
        P("fsdp"),
        P("fsdp", "tok"),
        P(),
        P(),
        P(),
        P(("fsdp", "tok"), None),
        P(("fsdp", "tok"), None),
        P(("fsdp", "tok"), None),
        P(("fsdp", "tok"), None),
    )
    out_specs = (P("fsdp", "tok", None), P("fsdp", "tok", None), P("fsdp", "tok", None))
    near = 2 if mesh.shape["tok"] <= 8 else 4
    return jax.shard_map(
        functools.partial(shards, near),
        mesh=mesh,
        in_specs=in_specs,
        out_specs=out_specs,
        check_vma=False,
    )
```

```python
import functools

import jax
import jax.numpy as jnp
from jax import lax
from jax.experimental import pallas as pl
from jax.experimental.pallas import tpu as pltpu
from jax.sharding import PartitionSpec as P

masked = -1e30
q_rows = 128
lanes = 128
slot_base = 32
mebibyte = 1024 * 1024
vmem_grants = {"attend": 60 * mebibyte}
vmem_grant = 16 * mebibyte


def fetch(pairs, sems):
    copies = [
        pltpu.make_async_copy(source, target, sems.at[at])
        for at, (source, target) in enumerate(pairs)
    ]
    for copy in copies:
        copy.start()
    return copies


def token_places(near):
    peers, me = lax.axis_size("tok"), lax.axis_index("tok")
    far_of = [lax.rem(me + peers - near * step, peers) for step in range(peers // near)]
    places = list(far_of)
    for turn in range(1, near):
        places += [
            one - lax.rem(one, near) + lax.rem(one + near - turn, near) for one in far_of
        ]
    return places


def fsdp_origins():
    count, me = lax.axis_size("fsdp"), lax.axis_index("fsdp")
    origins = [lax.rem(me + count - 2 * step, count) for step in range(count // 2)]
    return origins + [origin + 1 - 2 * lax.rem(origin, 2) for origin in origins]


def place_kernel(near, part_ref, out_ref, sems):
    places = token_places(near)
    rows, span = out_ref.shape[0] // len(places), part_ref.shape[0] // len(places)
    pairs = [
        (
            part_ref.at[pl.ds((at + 1) * span - rows, rows)],
            out_ref.at[pl.ds(pl.multiple_of(place * rows, rows), rows)],
        )
        for at, place in enumerate(places)
    ]
    for copy in fetch(pairs, sems):
        copy.wait()


def table_kernel(len_ref, bias_ref, bucket_ref, cache_out, new_out, cache_tab, new_tab, sems):
    heads, unused, reach = cache_tab.shape
    first_head = lax.axis_index("tok") * heads
    span = new_tab.shape[2]
    new_count = span // 2
    tiles = bucket_ref.shape[0]
    swap = lax.broadcasted_iota(jnp.int32, (lanes, lanes), 0) + lax.broadcasted_iota(
        jnp.int32, (lanes, lanes), 1
    )
    swap = (swap == lanes - 1).astype(jnp.bfloat16)
    buckets = bucket_ref[...].astype(jnp.float32).astype(jnp.bfloat16)
    turned = jnp.dot(buckets, swap, preferred_element_type=jnp.float32).astype(jnp.int32)
    row = jnp.concatenate([turned[at : at + 1, :] for at in reversed(range(tiles))], axis=1)
    row = jnp.broadcast_to(row, (8, reach))
    copies = []
    for h in range(heads):
        found = jnp.zeros((8, reach), jnp.float32)
        for bucket in range(bias_ref.shape[0]):
            found = jnp.where(row == bucket, bias_ref[bucket, first_head + h], found)
        after = jnp.full((8, new_count), masked, jnp.float32)
        bases = (
            pltpu.roll(found, len_ref[0] + (new_count - q_rows + 1), 1),
            pltpu.roll(jnp.concatenate([found[:, reach - new_count :], after], axis=1), span - q_rows + 1, 1),
        )
        for at, (base, tab, out) in enumerate(
            zip(bases, (cache_tab, new_tab), (cache_out, new_out))
        ):
            sublane = lax.broadcasted_iota(jnp.int32, base.shape, 0)
            for bit in (1, 2, 4):
                base = jnp.where((sublane & bit) != 0, pltpu.roll(base, bit, 1), base)
            for group in range(q_rows // 8):
                tab[h, group * 8 : (group + 1) * 8, :] = (
                    pltpu.roll(base, group * 8, 1) if group else base
                )
            copy = pltpu.make_async_copy(tab.at[h], out.at[h], sems.at[2 * h + at])
            copy.start()
            copies.append(copy)
    for copy in copies:
        copy.wait()


def attend_kernel(
    near,
    width,
    head_size,
    token_parts,
    weight_parts,
    len_ref,
    *refs,
):
    x_refs = refs[:token_parts]
    w_refs = refs[token_parts : token_parts + weight_parts]
    (
        cache_any,
        cache_tab_any,
        new_tab_any,
        out_ref,
        all_x,
        all_w,
        cache_ref,
        cache_tab,
        new_tab,
        q_ref,
        k_ref,
        v_ref,
        key_aug,
        val_aug,
        new_val_aug,
        sems,
    ) = refs[token_parts + weight_parts :]
    head_count = width // head_size
    peers = out_ref.shape[0]
    tok_rows = out_ref.shape[1] // 3
    new_count, full = q_ref.shape
    cache_rows = (cache_ref.shape[1] - 8) // 2
    cache_count = peers * cache_rows
    length = len_ref[0]
    pairs = [
        (
            x_refs[0].at[pl.ds(at * (x_refs[0].shape[0] // peers), tok_rows)],
            all_x.at[pl.ds(pl.multiple_of(place * tok_rows, tok_rows), tok_rows)],
        )
        for at, place in enumerate(token_places(near))
    ]
    pairs.append((w_refs[0], all_w))
    first = len(pairs)
    pairs += [(cache_any, cache_ref), (cache_tab_any, cache_tab), (new_tab_any, new_tab)]
    copies = fetch(pairs, sems)
    for copy in copies[:first]:
        copy.wait()
    made = jnp.dot(
        all_x[...],
        all_w[...],
        preferred_element_type=jnp.float32,
    ).astype(jnp.bfloat16)
    for part, ref in enumerate((q_ref, k_ref, v_ref)):
        piece = made[:, part * width : (part + 1) * width]
        if width < full:
            piece = jnp.concatenate(
                [piece, jnp.zeros((new_count, full - width), jnp.bfloat16)], axis=1
            )
        ref[...] = piece

    for copy in copies[first:]:
        copy.wait()
    told = cache_ref[:, 2 * cache_rows :, :].astype(jnp.float32)
    slots = jnp.concatenate(
        [
            told[peer, 0:1, :tok_rows] * slot_base + told[peer, 1:2, :tok_rows]
            for peer in range(peers)
        ],
        axis=1,
    ).astype(jnp.int32)
    slot_row = lax.broadcasted_iota(jnp.int32, (new_count, new_count), 0)
    deal = (slots == slot_row).astype(jnp.bfloat16)
    for part, ref in ((1, k_ref), (2, v_ref)):
        dealt = jnp.dot(deal, ref[...], preferred_element_type=jnp.float32).astype(jnp.bfloat16)
        for dest in range(peers):
            out_ref[dest, part * tok_rows : (part + 1) * tok_rows, :] = dealt[
                dest * tok_rows : (dest + 1) * tok_rows, :width
            ]

    old_keys = cache_ref[:, :cache_rows, :].reshape(cache_count, width)
    old_vals = cache_ref[:, cache_rows : 2 * cache_rows, :].reshape(cache_count, width)
    if width < full:
        blank = jnp.zeros((cache_count, full - width), jnp.bfloat16)
        old_keys = jnp.concatenate([old_keys, blank], axis=1)
        old_vals = jnp.concatenate([old_vals, blank], axis=1)
    key_row = lax.broadcasted_iota(jnp.int32, (cache_count, full), 0)
    key_lane = lax.broadcasted_iota(jnp.int32, (cache_count, full), 1)
    new_lane = lax.broadcasted_iota(jnp.int32, (new_count, full), 1)
    dead = jnp.where(key_row < length, 0.0, masked).astype(jnp.bfloat16)
    one = jnp.ones((), jnp.bfloat16)
    for h in range(head_count):
        spare = ((h + 1) * head_size) % full
        mine = (key_lane >= h * head_size) & (key_lane < (h + 1) * head_size)
        mine_new = (new_lane >= h * head_size) & (new_lane < (h + 1) * head_size)
        key_aug[h] = jnp.where(key_lane == spare, dead, old_keys)
        val_aug[h] = jnp.where(mine, old_vals, one)
        new_val_aug[h] = jnp.where(mine_new, v_ref[...], one)

    lane = lax.broadcasted_iota(jnp.int32, (q_rows, full), 1)
    per_dest = tok_rows
    for block in range(new_count // q_rows):
        q_here = q_ref[block * q_rows : (block + 1) * q_rows, :]
        start = new_count - q_rows - block * q_rows
        seen = (block + 1) * q_rows
        made = None
        for h in range(head_count):
            spare = ((h + 1) * head_size) % full
            mine = (lane >= h * head_size) & (lane < (h + 1) * head_size)
            q_new = jnp.where(mine, q_here, jnp.zeros((), jnp.bfloat16))
            q_old = jnp.where(lane == spare, one, q_new)
            s_old = lax.dot_general(
                q_old, key_aug[h], (((1,), (1,)), ((), ())), preferred_element_type=jnp.float32
            )
            s_new = lax.dot_general(
                q_new,
                k_ref[:seen, :],
                (((1,), (1,)), ((), ())),
                preferred_element_type=jnp.float32,
            )
            s_old = s_old + cache_tab[h, :, start : start + cache_count]
            s_new = s_new + new_tab[h, :, start : start + seen]
            peak = jnp.maximum(
                jnp.max(s_old, axis=1, keepdims=True), jnp.max(s_new, axis=1, keepdims=True)
            )
            p_old = jnp.exp(s_old - peak).astype(jnp.bfloat16)
            p_new = jnp.exp(s_new - peak).astype(jnp.bfloat16)
            total = jnp.dot(p_old, val_aug[h], preferred_element_type=jnp.float32) + jnp.dot(
                p_new, new_val_aug[h, :seen, :], preferred_element_type=jnp.float32
            )
            part = total / total[:, spare : spare + 1]
            made = part if made is None else jnp.where(mine, part, made)
        made = made.astype(jnp.bfloat16)
        for piece in range(q_rows // per_dest):
            out_ref[block * (q_rows // per_dest) + piece, :per_dest, :] = made[
                piece * per_dest : (piece + 1) * per_dest, :width
            ]


def finish_kernel(got_ref, states_ref, *refs):
    w_refs = refs[:-6]
    hidden_ref, keys_ref, values_ref, all_w, context, sems = refs[-6:]
    peers = got_ref.shape[0]
    rows, features = states_ref.shape
    depth = w_refs[0].shape[0]
    copies = fetch([(w_ref, all_w.at[part]) for part, w_ref in enumerate(w_refs)], sems)
    for part, ref in ((1, keys_ref), (2, values_ref)):
        ref[...] = jnp.concatenate(
            [got_ref[p, part * rows : (part + 1) * rows, :] for p in range(peers)], axis=1
        )
    context[...] = jnp.concatenate([got_ref[p, :rows, :] for p in range(peers)], axis=1)
    made = states_ref[...].astype(jnp.float32)
    for part, (copy, origin) in enumerate(zip(copies, fsdp_origins())):
        copy.wait()
        spot = pl.multiple_of(origin * depth, depth)
        made = made + jnp.dot(
            context[:, pl.ds(spot, depth)], all_w[part], preferred_element_type=jnp.float32
        )
    hidden_ref[...] = made.astype(jnp.bfloat16)


def vmem():
    return pl.BlockSpec(memory_space=pltpu.VMEM)


def hbm():
    return pl.BlockSpec(memory_space=pltpu.HBM)


def smem():
    return pl.BlockSpec(memory_space=pltpu.SMEM)


def call(kernel, outs, specs, scratch, name, flops, moved, kind=jnp.bfloat16, out_space=vmem):
    return pl.pallas_call(
        kernel,
        out_shape=[jax.ShapeDtypeStruct(shape, kind) for shape in outs],
        in_specs=specs,
        out_specs=[out_space() for unused in outs],
        scratch_shapes=scratch,
        name=name,
        cost_estimate=pl.CostEstimate(flops=flops, bytes_accessed=moved, transcendentals=0),
        compiler_params=pltpu.CompilerParams(vmem_limit_bytes=vmem_grants.get(name, vmem_grant)),
    )


def shards(
    near,
    states,
    cache_keys,
    cache_values,
    cache_len,
    token_slot,
    bucket_table,
    rel_bias,
    norm_gain,
    w_query,
    w_key,
    w_value,
    w_out,
):
    peers = lax.axis_size("tok")
    tokens = states[0]
    tok_rows, features = tokens.shape
    heads = rel_bias.shape[1]
    head_size = features // heads
    width = features // peers
    my_heads = width // head_size
    new_count = tok_rows * peers
    cache_rows = cache_keys.shape[1]

    fsdp_count = lax.axis_size("fsdp")
    far = peers // near

    def over_tok(parts, turns):
        return [lax.ppermute(part, "tok", turns) for part in parts]

    def far_turn(step):
        return [(t, (t + near * step) % peers) for t in range(peers)]

    def near_turn(step):
        return [(t, t - t % near + (t + step) % near) for t in range(peers)]

    def gather_fsdp(part):
        parts = [part]
        for step in range(1, fsdp_count // 2):
            turn = [(f, (f + 2 * step) % fsdp_count) for f in range(fsdp_count)]
            parts.append(lax.ppermute(part, "fsdp", turn))
        swap = [(f, f ^ 1) for f in range(fsdp_count)]
        return parts + [lax.ppermute(one, "fsdp", swap) for one in parts]

    sent_w = jnp.stack([w_query, w_key, w_value], axis=1).reshape(-1, 3, peers, width)
    sent_w = jnp.transpose(sent_w, (2, 0, 1, 3)).reshape(peers, -1, 3 * width)
    got_w = lax.all_to_all(sent_w, "tok", split_axis=0, concat_axis=0, tiled=True)

    reach = bucket_table.shape[0]
    shapes = [(my_heads, q_rows, reach), (my_heads, q_rows, 2 * new_count)]
    cache_tab, new_tab = call(
        table_kernel,
        shapes,
        [smem()] * 2 + [vmem()],
        [pltpu.VMEM(shape, jnp.float32) for shape in shapes]
        + [pltpu.SemaphoreType.DMA((2 * my_heads,))],
        "tables",
        0,
        4 * my_heads * q_rows * (reach + 2 * new_count),
        jnp.float32,
        hbm,
    )(
        cache_len,
        rel_bias,
        bucket_table.reshape(reach // lanes, lanes),
    )

    got_w, cache_tab, new_tab = lax.optimization_barrier((got_w, cache_tab, new_tab))
    my_w = [lax.all_gather(got_w.reshape(-1, 3 * width), "fsdp", axis=0, tiled=True)]

    wide_in = tokens.astype(jnp.float32)
    inverse = lax.rsqrt(jnp.mean(wide_in * wide_in, axis=-1, keepdims=True) + 1e-06)
    normed = (wide_in * inverse * norm_gain).astype(jnp.bfloat16)
    out_rows = w_out.shape[0]
    normed = jnp.concatenate([normed, w_out])
    parts = [normed] + [lax.ppermute(normed, "tok", far_turn(step)) for step in range(1, far)]
    for turn in range(1, near):
        parts += over_tok(parts[:far], near_turn(turn))

    *parts, weights = lax.optimization_barrier((*parts, my_w[0]))
    my_w = [weights]
    parts = [jnp.concatenate(parts)]

    def columns(rows):
        return jnp.transpose(rows.reshape(-1, peers, width), (1, 0, 2))

    slots = token_slot[0]
    note = jnp.zeros((8, width), jnp.bfloat16)
    note = note.at[0, :tok_rows].set((slots // slot_base).astype(jnp.bfloat16))
    note = note.at[1, :tok_rows].set((slots % slot_base).astype(jnp.bfloat16))
    sent_cache = jnp.concatenate(
        [
            columns(cache_keys[0]),
            columns(cache_values[0]),
            jnp.broadcast_to(note[None], (peers, 8, width)),
        ],
        axis=1,
    )
    cache = lax.all_to_all(sent_cache, "tok", split_axis=0, concat_axis=0, tiled=True)

    (out_tok,) = call(
        functools.partial(place_kernel, near),
        [(peers * out_rows, features)],
        [hbm()],
        [pltpu.SemaphoreType.DMA((peers,))],
        "place",
        0,
        4 * peers * out_rows * features,
    )(*parts)
    out_w = gather_fsdp(out_tok)

    full = max(width, lanes)
    cache_count = peers * cache_rows
    (sent,) = call(
        functools.partial(attend_kernel, near, width, head_size, len(parts), len(my_w)),
        [(peers, 3 * tok_rows, width)],
        [smem()] + [hbm()] * (len(parts) + len(my_w) + 3),
        [
            pltpu.VMEM((new_count, features), jnp.bfloat16),
            pltpu.VMEM((features, 3 * width), jnp.bfloat16),
            pltpu.VMEM(cache.shape, jnp.bfloat16),
            pltpu.VMEM(cache_tab.shape, jnp.float32),
            pltpu.VMEM(new_tab.shape, jnp.float32),
        ]
        + [pltpu.VMEM((new_count, full), jnp.bfloat16)] * 3
        + [
            pltpu.VMEM((my_heads, cache_count, full), jnp.bfloat16),
            pltpu.VMEM((my_heads, cache_count, full), jnp.bfloat16),
            pltpu.VMEM((my_heads, new_count, full), jnp.bfloat16),
            pltpu.SemaphoreType.DMA((peers + len(my_w) + 3,)),
        ],
        "attend",
        6 * new_count * features * width
        + 4 * my_heads * new_count * (new_count + cache_count) * full,
        2 * features * (new_count + 3 * width) + 4 * full * cache_count,
    )(cache_len, *parts, *my_w, cache, cache_tab, new_tab)

    got = lax.all_to_all(sent, "tok", split_axis=0, concat_axis=0, tiled=True)
    hidden, new_keys, new_values = call(
        finish_kernel,
        [(tok_rows, features)] * 3,
        [vmem()] * 2 + [hbm()] * len(out_w),
        [
            pltpu.VMEM((fsdp_count,) + out_tok.shape, jnp.bfloat16),
            pltpu.VMEM((tok_rows, features), jnp.bfloat16),
            pltpu.SemaphoreType.DMA((len(out_w),)),
        ],
        "finish",
        2 * tok_rows * features * features,
        2 * features * (features + 5 * tok_rows),
    )(got, tokens, *out_w)
    return (hidden[None], new_keys[None], new_values[None])


def solution(mesh):
    in_specs = (
        P("fsdp", "tok", None),
        P("fsdp", "tok", None),
        P("fsdp", "tok", None),
        P("fsdp"),
        P("fsdp", "tok"),
        P(),
        P(),
        P(),
        P(("fsdp", "tok"), None),
        P(("fsdp", "tok"), None),
        P(("fsdp", "tok"), None),
        P(("fsdp", "tok"), None),
    )
    out_specs = (P("fsdp", "tok", None), P("fsdp", "tok", None), P("fsdp", "tok", None))
    near = 2 if mesh.shape["tok"] <= 8 else 4
    return jax.shard_map(
        functools.partial(shards, near),
        mesh=mesh,
        in_specs=in_specs,
        out_specs=out_specs,
        check_vma=False,
    )
```

```python
import functools

import jax
import jax.numpy as jnp
from jax import lax
from jax.experimental import pallas as pl
from jax.experimental.pallas import tpu as pltpu
from jax.sharding import PartitionSpec as P

masked = -1e30
q_rows = 128
lanes = 128
slot_base = 32
mebibyte = 1024 * 1024
vmem_grants = {"attend": 24 * mebibyte}
vmem_grant = 16 * mebibyte


def fetch(pairs, sems):
    copies = [
        pltpu.make_async_copy(source, target, sems.at[at])
        for at, (source, target) in enumerate(pairs)
    ]
    for copy in copies:
        copy.start()
    return copies


def token_places(near):
    peers, me = lax.axis_size("tok"), lax.axis_index("tok")
    far_of = [lax.rem(me + peers - near * step, peers) for step in range(peers // near)]
    places = list(far_of)
    for turn in range(1, near):
        places += [
            one - lax.rem(one, near) + lax.rem(one + near - turn, near) for one in far_of
        ]
    return places


def fsdp_origins():
    count, me = lax.axis_size("fsdp"), lax.axis_index("fsdp")
    origins = [lax.rem(me + count - 2 * step, count) for step in range(count // 2)]
    return origins + [origin + 1 - 2 * lax.rem(origin, 2) for origin in origins]


def place_kernel(near, part_ref, out_ref, sems):
    places = token_places(near)
    rows, span = out_ref.shape[0] // len(places), part_ref.shape[0] // len(places)
    pairs = [
        (
            part_ref.at[pl.ds((at + 1) * span - rows, rows)],
            out_ref.at[pl.ds(pl.multiple_of(place * rows, rows), rows)],
        )
        for at, place in enumerate(places)
    ]
    for copy in fetch(pairs, sems):
        copy.wait()


def table_kernel(len_ref, bias_ref, bucket_ref, cache_tab, new_tab):
    heads, unused, reach = cache_tab.shape
    first_head = lax.axis_index("tok") * heads
    span = new_tab.shape[2]
    new_count = span // 2
    tiles = bucket_ref.shape[0]
    swap = lax.broadcasted_iota(jnp.int32, (lanes, lanes), 0) + lax.broadcasted_iota(
        jnp.int32, (lanes, lanes), 1
    )
    swap = (swap == lanes - 1).astype(jnp.bfloat16)
    buckets = bucket_ref[...].astype(jnp.float32).astype(jnp.bfloat16)
    turned = jnp.dot(buckets, swap, preferred_element_type=jnp.float32).astype(jnp.int32)
    row = jnp.concatenate([turned[at : at + 1, :] for at in reversed(range(tiles))], axis=1)
    row = jnp.broadcast_to(row, (8, reach))
    for h in range(heads):
        found = jnp.zeros((8, reach), jnp.float32)
        for bucket in range(bias_ref.shape[0]):
            found = jnp.where(row == bucket, bias_ref[bucket, first_head + h], found)
        after = jnp.full((8, new_count), masked, jnp.float32)
        bases = (
            pltpu.roll(found, len_ref[0] + (new_count - q_rows + 1), 1),
            pltpu.roll(jnp.concatenate([found[:, reach - new_count :], after], axis=1), span - q_rows + 1, 1),
        )
        for base, tab in zip(bases, (cache_tab, new_tab)):
            sublane = lax.broadcasted_iota(jnp.int32, base.shape, 0)
            for bit in (1, 2, 4):
                base = jnp.where((sublane & bit) != 0, pltpu.roll(base, bit, 1), base)
            tab[h] = base


def project_kernel(near, x_any, w_any, out_ref, all_x, all_w, sems):
    peers, width = lax.axis_size("tok"), w_any.shape[1]
    parts, new_count, full = out_ref.shape
    tok_rows, span = new_count // peers, x_any.shape[0] // peers
    pairs = [
        (
            x_any.at[pl.ds(at * span, tok_rows)],
            all_x.at[pl.ds(pl.multiple_of(place * tok_rows, tok_rows), tok_rows)],
        )
        for at, place in enumerate(token_places(near))
    ]
    pairs.append((w_any, all_w))
    for copy in fetch(pairs, sems):
        copy.wait()
    depth = all_w.shape[0] // (parts * peers * lax.axis_size("fsdp"))
    weights = all_w[...].reshape(-1, parts, depth, width)
    weights = jnp.concatenate(
        [weights[:, part].reshape(all_x.shape[1], width) for part in range(parts)], axis=1
    )
    made = jnp.dot(all_x[...], weights, preferred_element_type=jnp.float32).astype(jnp.bfloat16)
    for part in range(parts):
        piece = made[:, part * width : (part + 1) * width]
        if width < full:
            piece = jnp.concatenate(
                [piece, jnp.zeros((new_count, full - width), jnp.bfloat16)], axis=1
            )
        out_ref[part] = piece


def attend_kernel(
    width,
    head_size,
    len_ref,
    made_any,
    cache_any,
    cache_base,
    new_base,
    out_ref,
    made,
    cache_ref,
    cache_tab,
    new_tab,
    key_aug,
    val_aug,
    new_val_aug,
    sems,
):
    head_count = width // head_size
    peers = out_ref.shape[0]
    tok_rows = out_ref.shape[1] // 3
    new_count, full = made.shape[1:]
    cache_rows = (cache_ref.shape[1] - 8) // 2
    cache_count = peers * cache_rows
    length = len_ref[0]
    copies = fetch([(made_any, made), (cache_any, cache_ref)], sems)
    for base_ref, tab in ((cache_base, cache_tab), (new_base, new_tab)):
        for h in range(head_count):
            for group in range(q_rows // 8):
                tab[h, group * 8 : (group + 1) * 8, :] = (
                    pltpu.roll(base_ref[h], group * 8, 1) if group else base_ref[h]
                )
    q_ref, k_ref, v_ref = (made.at[part] for part in range(3))
    for copy in copies[:2]:
        copy.wait()

    told = cache_ref[:, 2 * cache_rows :, :].astype(jnp.float32)
    slots = jnp.concatenate(
        [
            told[peer, 0:1, :tok_rows] * slot_base + told[peer, 1:2, :tok_rows]
            for peer in range(peers)
        ],
        axis=1,
    ).astype(jnp.int32)
    slot_row = lax.broadcasted_iota(jnp.int32, (new_count, new_count), 0)
    deal = (slots == slot_row).astype(jnp.bfloat16)
    for part, ref in ((1, k_ref), (2, v_ref)):
        dealt = jnp.dot(deal, ref[...], preferred_element_type=jnp.float32).astype(jnp.bfloat16)
        for dest in range(peers):
            out_ref[dest, part * tok_rows : (part + 1) * tok_rows, :] = dealt[
                dest * tok_rows : (dest + 1) * tok_rows, :width
            ]

    old_keys = cache_ref[:, :cache_rows, :].reshape(cache_count, width)
    old_vals = cache_ref[:, cache_rows : 2 * cache_rows, :].reshape(cache_count, width)
    if width < full:
        blank = jnp.zeros((cache_count, full - width), jnp.bfloat16)
        old_keys = jnp.concatenate([old_keys, blank], axis=1)
        old_vals = jnp.concatenate([old_vals, blank], axis=1)
    key_row = lax.broadcasted_iota(jnp.int32, (cache_count, full), 0)
    key_lane = lax.broadcasted_iota(jnp.int32, (cache_count, full), 1)
    new_lane = lax.broadcasted_iota(jnp.int32, (new_count, full), 1)
    dead = jnp.where(key_row < length, 0.0, masked).astype(jnp.bfloat16)
    one = jnp.ones((), jnp.bfloat16)
    for h in range(head_count):
        spare = ((h + 1) * head_size) % full
        mine = (key_lane >= h * head_size) & (key_lane < (h + 1) * head_size)
        mine_new = (new_lane >= h * head_size) & (new_lane < (h + 1) * head_size)
        key_aug[h] = jnp.where(key_lane == spare, dead, old_keys)
        val_aug[h] = jnp.where(mine, old_vals, one)
        new_val_aug[h] = jnp.where(mine_new, v_ref[...], one)

    lane = lax.broadcasted_iota(jnp.int32, (q_rows, full), 1)
    per_dest = tok_rows
    for block in range(new_count // q_rows):
        q_here = q_ref[block * q_rows : (block + 1) * q_rows, :]
        start = new_count - q_rows - block * q_rows
        seen = (block + 1) * q_rows
        made = None
        for h in range(head_count):
            spare = ((h + 1) * head_size) % full
            mine = (lane >= h * head_size) & (lane < (h + 1) * head_size)
            q_new = jnp.where(mine, q_here, jnp.zeros((), jnp.bfloat16))
            q_old = jnp.where(lane == spare, one, q_new)
            s_old = lax.dot_general(
                q_old, key_aug[h], (((1,), (1,)), ((), ())), preferred_element_type=jnp.float32
            )
            s_new = lax.dot_general(
                q_new,
                k_ref[:seen, :],
                (((1,), (1,)), ((), ())),
                preferred_element_type=jnp.float32,
            )
            s_old = s_old + cache_tab[h, :, start : start + cache_count]
            s_new = s_new + new_tab[h, :, start : start + seen]
            peak = jnp.maximum(
                jnp.max(s_old, axis=1, keepdims=True), jnp.max(s_new, axis=1, keepdims=True)
            )
            p_old = jnp.exp(s_old - peak).astype(jnp.bfloat16)
            p_new = jnp.exp(s_new - peak).astype(jnp.bfloat16)
            total = jnp.dot(p_old, val_aug[h], preferred_element_type=jnp.float32) + jnp.dot(
                p_new, new_val_aug[h, :seen, :], preferred_element_type=jnp.float32
            )
            part = total / total[:, spare : spare + 1]
            made = part if made is None else jnp.where(mine, part, made)
        made = made.astype(jnp.bfloat16)
        for piece in range(q_rows // per_dest):
            out_ref[block * (q_rows // per_dest) + piece, :per_dest, :] = made[
                piece * per_dest : (piece + 1) * per_dest, :width
            ]


def finish_kernel(got_ref, states_ref, *refs):
    w_refs = refs[:-6]
    hidden_ref, keys_ref, values_ref, all_w, context, sems = refs[-6:]
    peers = got_ref.shape[0]
    rows, features = states_ref.shape
    depth = w_refs[0].shape[0]
    copies = fetch([(w_ref, all_w.at[part]) for part, w_ref in enumerate(w_refs)], sems)
    for part, ref in ((1, keys_ref), (2, values_ref)):
        ref[...] = jnp.concatenate(
            [got_ref[p, part * rows : (part + 1) * rows, :] for p in range(peers)], axis=1
        )
    context[...] = jnp.concatenate([got_ref[p, :rows, :] for p in range(peers)], axis=1)
    made = states_ref[...].astype(jnp.float32)
    for part, (copy, origin) in enumerate(zip(copies, fsdp_origins())):
        copy.wait()
        spot = pl.multiple_of(origin * depth, depth)
        made = made + jnp.dot(
            context[:, pl.ds(spot, depth)], all_w[part], preferred_element_type=jnp.float32
        )
    hidden_ref[...] = made.astype(jnp.bfloat16)


def vmem():
    return pl.BlockSpec(memory_space=pltpu.VMEM)


def hbm():
    return pl.BlockSpec(memory_space=pltpu.HBM)


def smem():
    return pl.BlockSpec(memory_space=pltpu.SMEM)


def call(kernel, outs, specs, scratch, name, flops, moved, kind=jnp.bfloat16, out_space=vmem):
    return pl.pallas_call(
        kernel,
        out_shape=[jax.ShapeDtypeStruct(shape, kind) for shape in outs],
        in_specs=specs,
        out_specs=[out_space() for unused in outs],
        scratch_shapes=scratch,
        name=name,
        cost_estimate=pl.CostEstimate(flops=flops, bytes_accessed=moved, transcendentals=0),
        compiler_params=pltpu.CompilerParams(vmem_limit_bytes=vmem_grants.get(name, vmem_grant)),
    )


def shards(
    near,
    states,
    cache_keys,
    cache_values,
    cache_len,
    token_slot,
    bucket_table,
    rel_bias,
    norm_gain,
    w_query,
    w_key,
    w_value,
    w_out,
):
    peers = lax.axis_size("tok")
    tokens = states[0]
    tok_rows, features = tokens.shape
    heads = rel_bias.shape[1]
    head_size = features // heads
    width = features // peers
    my_heads = width // head_size
    new_count = tok_rows * peers
    cache_rows = cache_keys.shape[1]

    fsdp_count = lax.axis_size("fsdp")
    far = peers // near

    def over_tok(parts, turns):
        return [lax.ppermute(part, "tok", turns) for part in parts]

    def far_turn(step):
        return [(t, (t + near * step) % peers) for t in range(peers)]

    def near_turn(step):
        return [(t, t - t % near + (t + step) % near) for t in range(peers)]

    def gather_fsdp(part):
        parts = [part]
        for step in range(1, fsdp_count // 2):
            turn = [(f, (f + 2 * step) % fsdp_count) for f in range(fsdp_count)]
            parts.append(lax.ppermute(part, "fsdp", turn))
        swap = [(f, f ^ 1) for f in range(fsdp_count)]
        return parts + [lax.ppermute(one, "fsdp", swap) for one in parts]

    def columns(rows):
        return jnp.transpose(rows.reshape(-1, peers, width), (1, 0, 2))

    sent_w = jnp.concatenate([columns(w_query), columns(w_key), columns(w_value)], axis=1)
    got_w = lax.all_to_all(sent_w, "tok", split_axis=0, concat_axis=0, tiled=True)

    reach = bucket_table.shape[0]
    cache_tab, new_tab = call(
        table_kernel,
        [(my_heads, 8, reach), (my_heads, 8, 2 * new_count)],
        [smem()] * 2 + [vmem()],
        [],
        "tables",
        0,
        32 * my_heads * (reach + 2 * new_count),
        jnp.float32,
    )(
        cache_len,
        rel_bias,
        bucket_table.reshape(reach // lanes, lanes),
    )

    got_w, cache_tab, new_tab = lax.optimization_barrier((got_w, cache_tab, new_tab))
    my_w = [lax.all_gather(got_w.reshape(-1, width), "fsdp", axis=0, tiled=True)]

    wide_in = tokens.astype(jnp.float32)
    inverse = lax.rsqrt(jnp.mean(wide_in * wide_in, axis=-1, keepdims=True) + 1e-06)
    normed = (wide_in * inverse * norm_gain).astype(jnp.bfloat16)
    out_rows = w_out.shape[0]
    normed = jnp.concatenate([normed, w_out])
    parts = [normed] + [lax.ppermute(normed, "tok", far_turn(step)) for step in range(1, far)]
    for turn in range(1, near):
        parts += over_tok(parts[:far], near_turn(turn))

    *parts, weights = lax.optimization_barrier((*parts, my_w[0]))
    my_w = [weights]
    parts = [jnp.concatenate(parts)]

    slots = token_slot[0]
    note = jnp.zeros((8, width), jnp.bfloat16)
    note = note.at[0, :tok_rows].set((slots // slot_base).astype(jnp.bfloat16))
    note = note.at[1, :tok_rows].set((slots % slot_base).astype(jnp.bfloat16))
    sent_cache = jnp.concatenate(
        [
            columns(cache_keys[0]),
            columns(cache_values[0]),
            jnp.broadcast_to(note[None], (peers, 8, width)),
        ],
        axis=1,
    )
    cache = lax.all_to_all(sent_cache, "tok", split_axis=0, concat_axis=0, tiled=True)

    (out_tok,) = call(
        functools.partial(place_kernel, near),
        [(peers * out_rows, features)],
        [hbm()],
        [pltpu.SemaphoreType.DMA((peers,))],
        "place",
        0,
        4 * peers * out_rows * features,
    )(*parts)
    out_w = gather_fsdp(out_tok)

    full = max(width, lanes)
    cache_count = peers * cache_rows
    (made,) = call(
        functools.partial(project_kernel, near),
        [(3, new_count, full)],
        [hbm()] * 2,
        [
            pltpu.VMEM((new_count, features), jnp.bfloat16),
            pltpu.VMEM((3 * features, width), jnp.bfloat16),
            pltpu.SemaphoreType.DMA((peers + 1,)),
        ],
        "project",
        6 * new_count * features * width,
        2 * features * (new_count + 3 * width),
    )(*parts, *my_w)
    (sent,) = call(
        functools.partial(attend_kernel, width, head_size),
        [(peers, 3 * tok_rows, width)],
        [smem()] + [hbm()] * 2 + [vmem()] * 2,
        [
            pltpu.VMEM((3, new_count, full), jnp.bfloat16),
            pltpu.VMEM(cache.shape, jnp.bfloat16),
            pltpu.VMEM((my_heads, q_rows, reach), jnp.float32),
            pltpu.VMEM((my_heads, q_rows, 2 * new_count), jnp.float32),
            pltpu.VMEM((my_heads, cache_count, full), jnp.bfloat16),
            pltpu.VMEM((my_heads, cache_count, full), jnp.bfloat16),
            pltpu.VMEM((my_heads, new_count, full), jnp.bfloat16),
            pltpu.SemaphoreType.DMA((2,)),
        ],
        "attend",
        4 * my_heads * new_count * (new_count + cache_count) * full,
        8 * full * cache_count,
    )(cache_len, made, cache, cache_tab, new_tab)

    got = lax.all_to_all(sent, "tok", split_axis=0, concat_axis=0, tiled=True)
    hidden, new_keys, new_values = call(
        finish_kernel,
        [(tok_rows, features)] * 3,
        [vmem()] * 2 + [hbm()] * len(out_w),
        [
            pltpu.VMEM((fsdp_count,) + out_tok.shape, jnp.bfloat16),
            pltpu.VMEM((tok_rows, features), jnp.bfloat16),
            pltpu.SemaphoreType.DMA((len(out_w),)),
        ],
        "finish",
        2 * tok_rows * features * features,
        2 * features * (features + 5 * tok_rows),
    )(got, tokens, *out_w)
    return (hidden[None], new_keys[None], new_values[None])


def solution(mesh):
    in_specs = (
        P("fsdp", "tok", None),
        P("fsdp", "tok", None),
        P("fsdp", "tok", None),
        P("fsdp"),
        P("fsdp", "tok"),
        P(),
        P(),
        P(),
        P(("fsdp", "tok"), None),
        P(("fsdp", "tok"), None),
        P(("fsdp", "tok"), None),
        P(("fsdp", "tok"), None),
    )
    out_specs = (P("fsdp", "tok", None), P("fsdp", "tok", None), P("fsdp", "tok", None))
    near = 2 if mesh.shape["tok"] <= 8 else 4
    return jax.shard_map(
        functools.partial(shards, near),
        mesh=mesh,
        in_specs=in_specs,
        out_specs=out_specs,
        check_vma=False,
    )
```

```python
import functools

import jax
import jax.numpy as jnp
from jax import lax
from jax.experimental import pallas as pl
from jax.experimental.pallas import tpu as pltpu
from jax.sharding import PartitionSpec as P

masked = -1e30
q_rows = 128
lanes = 128
slot_base = 32
mebibyte = 1024 * 1024
vmem_grants = {"attend": 24 * mebibyte, "open": 60 * mebibyte}
vmem_grant = 16 * mebibyte


def fetch(pairs, sems):
    copies = [
        pltpu.make_async_copy(source, target, sems.at[at])
        for at, (source, target) in enumerate(pairs)
    ]
    for copy in copies:
        copy.start()
    return copies


def tok_turns(count):
    turns = []
    bit = count // 2
    while bit:
        turns.append(bit)
        bit //= 2
    return turns


def token_places():
    masks = [0]
    for turn in tok_turns(lax.axis_size("tok")):
        masks += [mask + turn for mask in masks]
    me = lax.axis_index("tok")
    return [lax.bitwise_xor(me, jnp.int32(mask)) for mask in masks]


def fsdp_origins():
    count, me = lax.axis_size("fsdp"), lax.axis_index("fsdp")
    origins = [lax.rem(me + count - 2 * step, count) for step in range(count // 2)]
    return origins + [origin + 1 - 2 * lax.rem(origin, 2) for origin in origins]


def open_kernel(
    gain_ref, states_any, wq_any, wk_any, wv_any, wo_any, block_ref, out_ref, tokens, weights, sems
):
    peers, unused, width = out_ref.shape
    rows, depth = tokens.shape[0], weights.shape[1]
    sources = [(states_any.at[0], tokens), (wo_any, block_ref.at[rows:])]
    sources += [(any_ref, weights.at[at]) for at, any_ref in enumerate((wq_any, wk_any, wv_any))]
    copies = fetch(sources, sems)
    copies[0].wait()
    wide = tokens[...].astype(jnp.float32)
    inverse = lax.rsqrt(jnp.mean(wide * wide, axis=-1, keepdims=True) + 1e-06)
    block_ref[:rows, :] = (wide * inverse * gain_ref[...]).astype(jnp.bfloat16)
    for part in range(3):
        copies[2 + part].wait()
        for dest in range(peers):
            out_ref[dest, part * depth : (part + 1) * depth, :] = weights[
                part, :, dest * width : (dest + 1) * width
            ]
    copies[1].wait()


def place_kernel(part_ref, out_ref, sems):
    places = token_places()
    rows, span = out_ref.shape[0] // len(places), part_ref.shape[0] // len(places)
    pairs = [
        (
            part_ref.at[pl.ds((at + 1) * span - rows, rows)],
            out_ref.at[pl.ds(pl.multiple_of(place * rows, rows), rows)],
        )
        for at, place in enumerate(places)
    ]
    for copy in fetch(pairs, sems):
        copy.wait()


def table_kernel(len_ref, bias_ref, bucket_ref, cache_tab, new_tab):
    heads, unused, reach = cache_tab.shape
    first_head = lax.axis_index("tok") * heads
    span = new_tab.shape[2]
    new_count = span // 2
    tiles = bucket_ref.shape[0]
    swap = lax.broadcasted_iota(jnp.int32, (lanes, lanes), 0) + lax.broadcasted_iota(
        jnp.int32, (lanes, lanes), 1
    )
    swap = (swap == lanes - 1).astype(jnp.bfloat16)
    buckets = bucket_ref[...].astype(jnp.float32).astype(jnp.bfloat16)
    turned = jnp.dot(buckets, swap, preferred_element_type=jnp.float32).astype(jnp.int32)
    row = jnp.concatenate([turned[at : at + 1, :] for at in reversed(range(tiles))], axis=1)
    row = jnp.broadcast_to(row, (8, reach))
    for h in range(heads):
        found = jnp.zeros((8, reach), jnp.float32)
        for bucket in range(bias_ref.shape[0]):
            found = jnp.where(row == bucket, bias_ref[bucket, first_head + h], found)
        after = jnp.full((8, new_count), masked, jnp.float32)
        bases = (
            pltpu.roll(found, len_ref[0] + (new_count - q_rows + 1), 1),
            pltpu.roll(jnp.concatenate([found[:, reach - new_count :], after], axis=1), span - q_rows + 1, 1),
        )
        for base, tab in zip(bases, (cache_tab, new_tab)):
            sublane = lax.broadcasted_iota(jnp.int32, base.shape, 0)
            for bit in (1, 2, 4):
                base = jnp.where((sublane & bit) != 0, pltpu.roll(base, bit, 1), base)
            tab[h] = base


def project_kernel(x_any, w_any, out_ref, all_x, all_w, sems):
    peers, width = lax.axis_size("tok"), w_any.shape[1]
    parts, new_count, full = out_ref.shape
    tok_rows, span = new_count // peers, x_any.shape[0] // peers
    pairs = [
        (
            x_any.at[pl.ds(at * span, tok_rows)],
            all_x.at[pl.ds(pl.multiple_of(place * tok_rows, tok_rows), tok_rows)],
        )
        for at, place in enumerate(token_places())
    ]
    pairs.append((w_any, all_w))
    for copy in fetch(pairs, sems):
        copy.wait()
    depth = all_w.shape[0] // (parts * peers * lax.axis_size("fsdp"))
    weights = all_w[...].reshape(-1, parts, depth, width)
    weights = jnp.concatenate(
        [weights[:, part].reshape(all_x.shape[1], width) for part in range(parts)], axis=1
    )
    made = jnp.dot(all_x[...], weights, preferred_element_type=jnp.float32).astype(jnp.bfloat16)
    for part in range(parts):
        piece = made[:, part * width : (part + 1) * width]
        if width < full:
            piece = jnp.concatenate(
                [piece, jnp.zeros((new_count, full - width), jnp.bfloat16)], axis=1
            )
        out_ref[part] = piece


def attend_kernel(
    width,
    head_size,
    len_ref,
    made_any,
    cache_any,
    cache_base,
    new_base,
    out_ref,
    made,
    cache_ref,
    cache_tab,
    new_tab,
    key_aug,
    val_aug,
    new_val_aug,
    sems,
):
    head_count = width // head_size
    peers = out_ref.shape[0]
    tok_rows = out_ref.shape[1] // 3
    new_count, full = made.shape[1:]
    cache_rows = (cache_ref.shape[1] - 8) // 2
    cache_count = peers * cache_rows
    length = len_ref[0]
    copies = fetch([(made_any, made), (cache_any, cache_ref)], sems)
    for base_ref, tab in ((cache_base, cache_tab), (new_base, new_tab)):
        for h in range(head_count):
            for group in range(q_rows // 8):
                tab[h, group * 8 : (group + 1) * 8, :] = (
                    pltpu.roll(base_ref[h], group * 8, 1) if group else base_ref[h]
                )
    q_ref, k_ref, v_ref = (made.at[part] for part in range(3))
    for copy in copies[:2]:
        copy.wait()

    told = cache_ref[:, 2 * cache_rows :, :].astype(jnp.float32)
    slots = jnp.concatenate(
        [
            told[peer, 0:1, :tok_rows] * slot_base + told[peer, 1:2, :tok_rows]
            for peer in range(peers)
        ],
        axis=1,
    ).astype(jnp.int32)
    slot_row = lax.broadcasted_iota(jnp.int32, (new_count, new_count), 0)
    deal = (slots == slot_row).astype(jnp.bfloat16)
    for part, ref in ((1, k_ref), (2, v_ref)):
        dealt = jnp.dot(deal, ref[...], preferred_element_type=jnp.float32).astype(jnp.bfloat16)
        for dest in range(peers):
            out_ref[dest, part * tok_rows : (part + 1) * tok_rows, :] = dealt[
                dest * tok_rows : (dest + 1) * tok_rows, :width
            ]

    old_keys = cache_ref[:, :cache_rows, :].reshape(cache_count, width)
    old_vals = cache_ref[:, cache_rows : 2 * cache_rows, :].reshape(cache_count, width)
    if width < full:
        blank = jnp.zeros((cache_count, full - width), jnp.bfloat16)
        old_keys = jnp.concatenate([old_keys, blank], axis=1)
        old_vals = jnp.concatenate([old_vals, blank], axis=1)
    key_row = lax.broadcasted_iota(jnp.int32, (cache_count, full), 0)
    key_lane = lax.broadcasted_iota(jnp.int32, (cache_count, full), 1)
    new_lane = lax.broadcasted_iota(jnp.int32, (new_count, full), 1)
    dead = jnp.where(key_row < length, 0.0, masked).astype(jnp.bfloat16)
    one = jnp.ones((), jnp.bfloat16)
    for h in range(head_count):
        spare = ((h + 1) * head_size) % full
        mine = (key_lane >= h * head_size) & (key_lane < (h + 1) * head_size)
        mine_new = (new_lane >= h * head_size) & (new_lane < (h + 1) * head_size)
        key_aug[h] = jnp.where(key_lane == spare, dead, old_keys)
        val_aug[h] = jnp.where(mine, old_vals, one)
        new_val_aug[h] = jnp.where(mine_new, v_ref[...], one)

    lane = lax.broadcasted_iota(jnp.int32, (q_rows, full), 1)
    turn_lhs = (((1,), (1,)), ((), ()))
    group = min(2, new_count // q_rows)
    for first in range(0, new_count // q_rows, group):
        blocks = range(first, first + group)
        q_here = [q_ref[block * q_rows : (block + 1) * q_rows, :] for block in blocks]
        made_here = [None] * group
        for h in range(head_count):
            spare = ((h + 1) * head_size) % full
            mine = (lane >= h * head_size) & (lane < (h + 1) * head_size)
            q_new = [jnp.where(mine, q, jnp.zeros((), jnp.bfloat16)) for q in q_here]
            q_old = jnp.concatenate([jnp.where(lane == spare, one, q) for q in q_new])
            s_all = lax.dot_general(
                q_old, key_aug[h], turn_lhs, preferred_element_type=jnp.float32
            )
            p_all, fresh = [], []
            for at, block in enumerate(blocks):
                start = new_count - q_rows - block * q_rows
                seen = (block + 1) * q_rows
                s_old = s_all[at * q_rows : (at + 1) * q_rows]
                s_old = s_old + cache_tab[h, :, start : start + cache_count]
                s_new = lax.dot_general(
                    q_new[at], k_ref[:seen, :], turn_lhs, preferred_element_type=jnp.float32
                )
                s_new = s_new + new_tab[h, :, start : start + seen]
                peak = jnp.maximum(
                    jnp.max(s_old, axis=1, keepdims=True), jnp.max(s_new, axis=1, keepdims=True)
                )
                p_all.append(jnp.exp(s_old - peak).astype(jnp.bfloat16))
                p_new = jnp.exp(s_new - peak).astype(jnp.bfloat16)
                fresh.append(
                    jnp.dot(p_new, new_val_aug[h, :seen, :], preferred_element_type=jnp.float32)
                )
            totals = jnp.dot(
                jnp.concatenate(p_all), val_aug[h], preferred_element_type=jnp.float32
            )
            for at in range(group):
                total = totals[at * q_rows : (at + 1) * q_rows] + fresh[at]
                part = total / total[:, spare : spare + 1]
                made_here[at] = part if h == 0 else jnp.where(mine, part, made_here[at])
        for block, ready in zip(blocks, made_here):
            ready = ready.astype(jnp.bfloat16)
            for piece in range(q_rows // tok_rows):
                out_ref[block * (q_rows // tok_rows) + piece, :tok_rows, :] = ready[
                    piece * tok_rows : (piece + 1) * tok_rows, :width
                ]


def finish_kernel(got_ref, states_ref, *refs):
    w_refs = refs[:-6]
    hidden_ref, keys_ref, values_ref, all_w, context, sems = refs[-6:]
    peers = got_ref.shape[0]
    rows, features = states_ref.shape
    depth = w_refs[0].shape[0]
    copies = fetch([(w_ref, all_w.at[part]) for part, w_ref in enumerate(w_refs)], sems)
    for part, ref in ((1, keys_ref), (2, values_ref)):
        ref[...] = jnp.concatenate(
            [got_ref[p, part * rows : (part + 1) * rows, :] for p in range(peers)], axis=1
        )
    context[...] = jnp.concatenate([got_ref[p, :rows, :] for p in range(peers)], axis=1)
    made = states_ref[...].astype(jnp.float32)
    for part, (copy, origin) in enumerate(zip(copies, fsdp_origins())):
        copy.wait()
        spot = pl.multiple_of(origin * depth, depth)
        made = made + jnp.dot(
            context[:, pl.ds(spot, depth)], all_w[part], preferred_element_type=jnp.float32
        )
    hidden_ref[...] = made.astype(jnp.bfloat16)


def vmem():
    return pl.BlockSpec(memory_space=pltpu.VMEM)


def hbm():
    return pl.BlockSpec(memory_space=pltpu.HBM)


def smem():
    return pl.BlockSpec(memory_space=pltpu.SMEM)


def call(kernel, outs, specs, scratch, name, flops, moved, kind=jnp.bfloat16, out_space=vmem):
    return pl.pallas_call(
        kernel,
        out_shape=[jax.ShapeDtypeStruct(shape, kind) for shape in outs],
        in_specs=specs,
        out_specs=[out_space() for unused in outs],
        scratch_shapes=scratch,
        name=name,
        cost_estimate=pl.CostEstimate(flops=flops, bytes_accessed=moved, transcendentals=0),
        compiler_params=pltpu.CompilerParams(vmem_limit_bytes=vmem_grants.get(name, vmem_grant)),
    )


def shards(
    states,
    cache_keys,
    cache_values,
    cache_len,
    token_slot,
    bucket_table,
    rel_bias,
    norm_gain,
    w_query,
    w_key,
    w_value,
    w_out,
):
    peers = lax.axis_size("tok")
    tokens = states[0]
    tok_rows, features = tokens.shape
    heads = rel_bias.shape[1]
    head_size = features // heads
    width = features // peers
    my_heads = width // head_size
    new_count = tok_rows * peers
    cache_rows = cache_keys.shape[1]

    fsdp_count = lax.axis_size("fsdp")

    def gather_fsdp(part):
        parts = [part]
        for step in range(1, fsdp_count // 2):
            turn = [(f, (f + 2 * step) % fsdp_count) for f in range(fsdp_count)]
            parts.append(lax.ppermute(part, "fsdp", turn))
        swap = [(f, f ^ 1) for f in range(fsdp_count)]
        return parts + [lax.ppermute(one, "fsdp", swap) for one in parts]

    def columns(rows):
        return jnp.transpose(rows.reshape(-1, peers, width), (1, 0, 2))

    depth, out_rows = w_query.shape[0], w_out.shape[0]
    block, sent_w = call(
        open_kernel,
        [(tok_rows + out_rows, features), (peers, 3 * depth, width)],
        [vmem()] + [hbm()] * 5,
        [
            pltpu.VMEM((tok_rows, features), jnp.bfloat16),
            pltpu.VMEM((3, depth, features), jnp.bfloat16),
            pltpu.SemaphoreType.DMA((5,)),
        ],
        "open",
        0,
        14 * features * depth,
    )(norm_gain.reshape(1, features), states, w_query, w_key, w_value, w_out)
    got_w = lax.all_to_all(sent_w, "tok", split_axis=0, concat_axis=0, tiled=True)

    my_w = [lax.all_gather(got_w.reshape(-1, width), "fsdp", axis=0, tiled=True)]

    reach = bucket_table.shape[0]
    cache_tab, new_tab = call(
        table_kernel,
        [(my_heads, 8, reach), (my_heads, 8, 2 * new_count)],
        [smem()] * 2 + [vmem()],
        [],
        "tables",
        0,
        32 * my_heads * (reach + 2 * new_count),
        jnp.float32,
    )(
        cache_len,
        rel_bias,
        bucket_table.reshape(reach // lanes, lanes),
    )

    slots = token_slot[0]
    note = jnp.zeros((8, width), jnp.bfloat16)
    note = note.at[0, :tok_rows].set((slots // slot_base).astype(jnp.bfloat16))
    note = note.at[1, :tok_rows].set((slots % slot_base).astype(jnp.bfloat16))
    sent_cache = jnp.concatenate(
        [
            columns(cache_keys[0]),
            columns(cache_values[0]),
            jnp.broadcast_to(note[None], (peers, 8, width)),
        ],
        axis=1,
    )

    parts = [block]
    for turn in tok_turns(peers):
        pairs = [(t, t ^ turn) for t in range(peers)]
        parts += [lax.ppermute(part, "tok", pairs) for part in parts]
        if len(parts) == 2:
            parts[1], cache_tab, new_tab = lax.optimization_barrier(
                (parts[1], cache_tab, new_tab)
            )

    *parts, weights = lax.optimization_barrier((*parts, my_w[0]))
    my_w = [weights]
    parts = [jnp.concatenate(parts)]

    cache = lax.all_to_all(sent_cache, "tok", split_axis=0, concat_axis=0, tiled=True)

    (out_tok,) = call(
        place_kernel,
        [(peers * out_rows, features)],
        [hbm()],
        [pltpu.SemaphoreType.DMA((peers,))],
        "place",
        0,
        4 * peers * out_rows * features,
    )(*parts)
    out_w = gather_fsdp(out_tok)

    full = max(width, lanes)
    cache_count = peers * cache_rows
    (made,) = call(
        project_kernel,
        [(3, new_count, full)],
        [hbm()] * 2,
        [
            pltpu.VMEM((new_count, features), jnp.bfloat16),
            pltpu.VMEM((3 * features, width), jnp.bfloat16),
            pltpu.SemaphoreType.DMA((peers + 1,)),
        ],
        "project",
        6 * new_count * features * width,
        2 * features * (new_count + 3 * width),
    )(*parts, *my_w)
    (sent,) = call(
        functools.partial(attend_kernel, width, head_size),
        [(peers, 3 * tok_rows, width)],
        [smem()] + [hbm()] * 2 + [vmem()] * 2,
        [
            pltpu.VMEM((3, new_count, full), jnp.bfloat16),
            pltpu.VMEM(cache.shape, jnp.bfloat16),
            pltpu.VMEM((my_heads, q_rows, reach), jnp.float32),
            pltpu.VMEM((my_heads, q_rows, 2 * new_count), jnp.float32),
            pltpu.VMEM((my_heads, cache_count, full), jnp.bfloat16),
            pltpu.VMEM((my_heads, cache_count, full), jnp.bfloat16),
            pltpu.VMEM((my_heads, new_count, full), jnp.bfloat16),
            pltpu.SemaphoreType.DMA((2,)),
        ],
        "attend",
        4 * my_heads * new_count * (new_count + cache_count) * full,
        8 * full * cache_count,
    )(cache_len, made, cache, cache_tab, new_tab)

    got = lax.all_to_all(sent, "tok", split_axis=0, concat_axis=0, tiled=True)
    hidden, new_keys, new_values = call(
        finish_kernel,
        [(tok_rows, features)] * 3,
        [vmem()] * 2 + [hbm()] * len(out_w),
        [
            pltpu.VMEM((fsdp_count,) + out_tok.shape, jnp.bfloat16),
            pltpu.VMEM((tok_rows, features), jnp.bfloat16),
            pltpu.SemaphoreType.DMA((len(out_w),)),
        ],
        "finish",
        2 * tok_rows * features * features,
        2 * features * (features + 5 * tok_rows),
    )(got, tokens, *out_w)
    return (hidden[None], new_keys[None], new_values[None])


def solution(mesh):
    in_specs = (
        P("fsdp", "tok", None),
        P("fsdp", "tok", None),
        P("fsdp", "tok", None),
        P("fsdp"),
        P("fsdp", "tok"),
        P(),
        P(),
        P(),
        P(("fsdp", "tok"), None),
        P(("fsdp", "tok"), None),
        P(("fsdp", "tok"), None),
        P(("fsdp", "tok"), None),
    )
    out_specs = (P("fsdp", "tok", None), P("fsdp", "tok", None), P("fsdp", "tok", None))
    return jax.shard_map(
        shards,
        mesh=mesh,
        in_specs=in_specs,
        out_specs=out_specs,
        check_vma=False,
    )
```
